32 devices in a mesh: strip: 8 (over z, x), period: 4 (over y, core).
Axes of the slice: x: 2, y: 2, z: 4, core: 2. Of those that a mesh axis runs over, the one named last changes fastest.
Arguments:
- u_start: float32 [8, 16, 64, 128], P('strip', 'period'), may hold values from 0 to 0.02
- dual_prec: float32 [5, 8, 16, 64, 128], P(None, 'strip', 'period'), may hold values from 0 to 0.5
- dual_bound: float32 [8, 16, 64, 128], P('strip', 'period'), may hold values from 0 to 0.5
- dual_cap: float32 [16], P('period'), may hold values from 0 to 2
- capacity: float32 [16], P('period'), may hold values from 0.005 to 0.03
- block_value: float32 [8, 64, 128], P('strip'), may hold values from -6 to 6
- ton_class: int32 [8, 64, 128], P('strip'), may hold values from 0 to 7
- density: float32 [8], replicated, may hold values from 1 to 3
- slope_code: int32 [8, 128], P('strip'), may hold values from 0 to 15
- omega_start: float32 [1], replicated, may hold values from 0.5 to 2
Outputs:
- mined_share: float32 [8, 16, 64, 128], P('strip', 'period')
- arc_prices: float32 [5, 8, 16, 64, 128], P(None, 'strip', 'period')
- bound_prices: float32 [8, 16, 64, 128], P('strip', 'period')
- capacity_prices: float32 [16], P('period')
- primal_weight: float32 [1], replicated
The draws below stay inside these ranges and needn't reach their ends.
All inputs are finite; a program needn't handle non-finite values.
Results may differ from the reference program's by a relative error of at most 0.0001.
Values sent between devices are 32-bit elements; how exact they have to be, the bound alone decides.
A program may use at most 64 MiB of HBM per device.

```python
import math
import jax
import jax.numpy as jnp
from jax import lax

NY = 128
NZ = 64
NARCS = 5
NCLASS = 8
OUTER = 2
INNER = 3
NX = 8
NP = 16


def draw_ton_class(key, part):
    base_class = jax.random.randint(key, (NX, NZ, NY), 0, NCLASS // 2)
    rising = jnp.arange(NX) * (NCLASS // 2 + 1) // NX
    return (base_class + rising[:, None, None]).astype(jnp.int32)


def touch_ends(array, key, smallest, top_value):
    shape = array.shape
    spot = [jax.random.randint(jax.random.fold_in(key, axis), (), 0, shape[axis]) for axis in range(len(shape))]
    array = array.at[tuple(spot)].set(smallest)
    longest = shape.index(max(shape))
    spot[longest] = (spot[longest] + 1) % shape[longest]
    return array.at[tuple(spot)].set(top_value)


def block_scale(key, extent, shards, least, high):
    level = 1.0
    for dim, parts in shards:
        draws = jax.random.uniform(jax.random.fold_in(jax.random.fold_in(key, 6), dim), (parts,), jnp.float32, least / len(shards), high / len(shards))
        level = level * jnp.repeat(jnp.exp(draws), extent[dim] // parts).reshape((-1,) + (1,) * (len(extent) - 1 - dim))
    return level


def bell_draw(key, extent, scale, most, split=(), held_as=jnp.bfloat16):
    values = jax.random.normal(key, extent, jnp.float32) * scale
    if len(split) > 0:
        values = block_scale(key, extent, split, -0.22, 0.18) * values
    return jnp.clip(values, min=-most, max=most).astype(held_as)


def setup_inputs(seed: int = 0) -> dict:
    splits = jax.random.split(jax.random.key(seed), 11)
    return {
        "u_start": jnp.clip(0.02 * jax.random.uniform(splits[0], (NX, NP, NZ, NY), jnp.float32) ** block_scale(splits[0], (NX, NP, NZ, NY), ((0, 8), (1, 4)), -0.2, 0.2), 0.0, 0.02),
        "dual_prec": jnp.clip(0.5 * jax.random.uniform(splits[1], (NARCS, NX, NP, NZ, NY), jnp.float32) ** block_scale(splits[1], (NARCS, NX, NP, NZ, NY), ((1, 8), (2, 4)), -0.2, 0.2), 0.0, 0.5),
        "dual_bound": jnp.clip(0.5 * jax.random.uniform(splits[2], (NX, NP, NZ, NY), jnp.float32) ** block_scale(splits[2], (NX, NP, NZ, NY), ((0, 8), (1, 4)), -0.2, 0.2), 0.0, 0.5),
        "dual_cap": jnp.clip(2.0 * jax.random.uniform(splits[3], (NP,), jnp.float32) ** block_scale(splits[3], (NP,), ((0, 4),), -0.2, 0.2), 0.0, 2.0),
        "capacity": jnp.clip(0.005 + 0.024999999 * jax.random.uniform(splits[4], (NP,), jnp.float32) ** block_scale(splits[4], (NP,), ((0, 4),), -0.2, 0.2), 0.005, 0.03),
        "block_value": bell_draw(splits[5], (NX, NZ, NY), 1.0, 6.0, ((0, 8),), jnp.float32),
        "ton_class": draw_ton_class(jax.random.fold_in(splits[10], 71), 0),
        "density": jnp.clip(jnp.exp(jax.random.uniform(splits[7], (NCLASS,), jnp.float32, math.log(1.0), math.log(3.0))), 1.0, 3.0),
        "slope_code": touch_ends(jax.random.randint(splits[8], (NX, NY), 0, 16), jax.random.fold_in(splits[8], 1), 0, 15).astype(jnp.int32),
        "omega_start": jnp.clip(jnp.exp(jax.random.uniform(splits[9], (1,), jnp.float32, math.log(0.5), math.log(2.0))), 0.5, 2.0),
    }


ARC_OFFSETS = ((0, 0), (1, 0), (-1, 0), (0, 1), (0, -1))
RATE = math.log(1.1) / 12.0
EPS = 1e-06
SLOPE = 11.0

def arc_masks(code_rows, first_row, total_rows, depth_cells, across):
    row_ids = (first_row + jnp.arange(code_rows.shape[0]))[:, None, None]
    depth_ids = jnp.arange(depth_cells)[None, :, None]
    col_ids = jnp.arange(across)[None, None, :]
    pattern = code_rows[:, None, :]
    mask_list = []
    for arc_index, (step_x, step_y) in enumerate(ARC_OFFSETS):
        inside = (row_ids >= 0) & (row_ids < total_rows) & (row_ids + step_x >= 0) & (row_ids + step_x < total_rows)
        inside = inside & (col_ids + step_y >= 0) & (col_ids + step_y < across) & (depth_ids >= 1)
        if arc_index > 0:
            inside = inside & (pattern // 2 ** (arc_index - 1) % 2 == 1)
        mask_list.append(inside.astype(jnp.float32))
    return jnp.stack(mask_list)

def tonnage(ton_class, density):
    class_ids = jnp.arange(density.shape[0])
    class_table = (1.0 + class_ids.astype(jnp.float32)) * density
    onehot = (class_ids[:, None, None, None] == ton_class[None]).astype(jnp.float32)
    return jnp.einsum('k,kxzy->xzy', class_table, onehot, precision=lax.Precision.HIGHEST)

def upper_cell(values_in, step_y):
    depth_cells = values_in.shape[2]
    across = values_in.shape[3]
    padded = jnp.pad(values_in, ((0, 0), (0, 0), (1, 0), (1, 1)))
    return padded[:, :, 0:depth_cells, 1 + step_y:1 + step_y + across]

def lower_cell(values_in, step_y):
    depth_cells = values_in.shape[2]
    across = values_in.shape[3]
    padded = jnp.pad(values_in, ((0, 0), (0, 0), (0, 1), (1, 1)))
    return padded[:, :, 1:depth_cells + 1, 1 - step_y:1 - step_y + across]

def adjoint(arc_duals, from_left, from_right, bound_duals):
    result = lax.optimization_barrier(jnp.sum(arc_duals, axis=0)) + bound_duals
    for arc_index, (step_x, step_y) in enumerate(ARC_OFFSETS):
        source = arc_duals[arc_index]
        if step_x == 1:
            source = jnp.concatenate([from_left, source[:-1]], axis=0)
        elif step_x == -1:
            source = jnp.concatenate([source[1:], from_right], axis=0)
        result = result - lower_cell(source, step_y)
    return result

def reference(u_start, dual_prec, dual_bound, dual_cap, capacity, block_value, ton_class, density, slope_code, omega_start):
    arc_active = arc_masks(slope_code, 0, NX, NZ, NY)[:, :, None]
    tonnage_grid = tonnage(ton_class, density)
    tons_col = tonnage_grid[:, None]
    tons_all = jnp.sum(tonnage_grid)
    blocks_all = float(NX * NY * NZ)
    root_blocks = math.sqrt(blocks_all)
    period_ids = jnp.arange(NP).astype(jnp.float32)[None, :, None, None]
    profit = block_value[:, None] * jnp.exp(-RATE * period_ids)
    zero_rim = jnp.zeros((1, NP, NZ, NY), jnp.float32)
    primal = u_start
    arc_duals = dual_prec * arc_active
    bound_duals = dual_bound
    cap_duals = dual_cap
    weight = omega_start[0]
    for restart in range(OUTER):
        primal_first, duals_first, bound_first, cap_first = (primal, arc_duals, bound_duals, cap_duals)
        primal_sum = jnp.zeros_like(primal)
        duals_sum = jnp.zeros_like(arc_duals)
        bound_sum = jnp.zeros_like(bound_duals)
        cap_sum = jnp.zeros_like(cap_duals)
        for sweep_index in range(INNER):
            gradient_x = adjoint(arc_duals, zero_rim, zero_rim, bound_duals)
            gradient_u = jnp.flip(jnp.cumsum(jnp.flip(gradient_x, 1), axis=1), 1) + tons_col * cap_duals[None, :, None, None] / root_blocks
            step_primal = 1.0 / (weight * (SLOPE * (NP - period_ids) + tons_col / root_blocks))
            primal_new = jnp.maximum(primal - step_primal * (gradient_u - profit), 0.0)
            extrapolated = 2.0 * primal_new - primal
            cumulative = jnp.cumsum(extrapolated, axis=1)
            padded = jnp.pad(cumulative, ((1, 1), (0, 0), (0, 0), (0, 0)))
            step_prec = weight / (2.0 * (period_ids + 1.0))
            step_bound = weight / (period_ids + 1.0)
            new_list = []
            for arc_index, (step_x, step_y) in enumerate(ARC_OFFSETS):
                ahead_cells = upper_cell(padded[1 + step_x:1 + step_x + NX], step_y)
                new_list.append(jnp.maximum(arc_duals[arc_index] + step_prec * (cumulative - ahead_cells), 0.0) * arc_active[arc_index])
            duals_new = jnp.stack(new_list)
            bound_new = jnp.maximum(bound_duals + step_bound * (cumulative - 1.0), 0.0)
            row_total = jnp.einsum('xzy,xtzy->t', tonnage_grid, extrapolated, precision=lax.Precision.HIGHEST)
            cap_new = jnp.maximum(cap_duals + weight * (row_total - blocks_all * capacity) / tons_all, 0.0)
            primal_sum = primal_sum + primal_new
            duals_sum = duals_sum + duals_new
            bound_sum = bound_sum + bound_new
            cap_sum = cap_sum + cap_new
            primal, arc_duals, bound_duals, cap_duals = (primal_new, duals_new, bound_new, cap_new)
        primal = primal_sum / INNER
        arc_duals = duals_sum / INNER
        bound_duals = bound_sum / INNER
        cap_duals = cap_sum / INNER
        primal_move = jnp.sum((primal - primal_first) ** 2)
        dual_move = jnp.sum((arc_duals - duals_first) ** 2) + jnp.sum((bound_duals - bound_first) ** 2) + jnp.sum((cap_duals - cap_first) ** 2)
        weight = jnp.sqrt(weight * jnp.sqrt((dual_move + EPS) / (primal_move + EPS)))
    return (primal, arc_duals, bound_duals, cap_duals, jnp.reshape(weight, (1,)))
```

```python
import functools
import math

import jax
import jax.numpy as jnp
from jax import lax
from jax.experimental import pallas as pl
from jax.experimental.pallas import tpu as pltpu
from jax.sharding import PartitionSpec as P

OUTER = 2
INNER = 3
STEPS = OUTER * INNER
RATE = math.log(1.1) / 12.0
EPS = 1e-06
SLOPE = 11.0
MESH = pl.DeviceIdType.MESH


def kernel(
    NS, NPD, T, Z, Y, R,
    u_ref, prec_ref, bound_ref, cap_ref, capacity_ref, bv_ref, tc_ref, dens_ref, slope_ref, om_ref,
    u_out, prec_out, bound_out, cap_out, w_out,
    uf, uc, us, bf, bc, bs, fa, ca, sa, act, ton, tb, tl, cb, ex0,
    xs, xr, es, er, as_, ar, rs, rb, ps, pb, slr,
    ini_s, ini_r, xs_s, xs_r, e_s, e_r, a_s, a_r, r_s, r_r, p_s, p_r,
):
    me = lax.axis_index("strip")
    pe = lax.axis_index("period")
    total_rows = NS
    total_periods = NPD * T
    blocks_all = float(total_rows * Z * Y)
    root_blocks = math.sqrt(blocks_all)
    sends = []

    barrier = pltpu.get_barrier_semaphore()
    for k in range(1, NS):
        pl.semaphore_signal(barrier, inc=1, device_id={"strip": lax.rem(me + k, NS)}, device_id_type=MESH)
    for k in range(1, NPD):
        pl.semaphore_signal(barrier, inc=1, device_id={"period": lax.rem(pe + k, NPD)}, device_id_type=MESH)
    pl.semaphore_wait(barrier, NS + NPD - 2)

    has = (me < NS - 1, me > 0)
    gets = (me > 0, me < NS - 1)
    to = (me + 1, me - 1)

    def remote(src, dst, ss, rr, dev):
        return pltpu.make_async_remote_copy(
            src_ref=src, dst_ref=dst, send_sem=ss, recv_sem=rr, device_id=dev, device_id_type=MESH
        )

    def ini_copy(d, what):
        if what == 0:
            return remote(prec_ref.at[1 + d, 0], fa.at[5 + d], ini_s.at[d, 0], ini_r.at[d, 0], {"strip": to[d]})
        return remote(slope_ref, slr.at[d], ini_s.at[d, 1], ini_r.at[d, 1], {"strip": to[d]})

    def x_copy(d, part, s):
        lo, size = (1, T - 1) if part == 0 else (0, 1)
        return remote(
            xs.at[s, pl.ds(lo, size)], xr.at[d, s, pl.ds(lo, size)],
            xs_s.at[d, part, s], xs_r.at[d, part, s], {"strip": to[d]},
        )

    def e_copy(k, s):
        return remote(es.at[s], er.at[s, k - 1], e_s.at[s, k - 1], e_r.at[s, k - 1], {"period": pe + k})

    def a_copy(k, s):
        return remote(as_.at[s], ar.at[s, k - 1], a_s.at[s, k - 1], a_r.at[s, k - 1], {"period": pe - k})

    def r_copy(k, slot):
        return remote(
            rs.at[slot], rb.at[slot, me], r_s.at[slot, k - 1], r_r.at[slot, k - 1],
            {"strip": lax.rem(me + k, NS)},
        )

    def p_copy(k, slot):
        return remote(
            ps.at[slot], pb.at[slot, pe], p_s.at[slot, k - 1], p_r.at[slot, k - 1],
            {"period": lax.rem(pe + k, NPD)},
        )

    def start(cond, copy):
        def go():
            copy.start()
        if cond is None:
            go()
        else:
            pl.when(cond)(go)
        sends.append((cond, copy))

    def wait_recv(cond, copy):
        if cond is None:
            copy.wait_recv()
        else:
            pl.when(cond)(lambda: copy.wait_recv())

    def reduce_start(slot, value):
        rs[slot] = value
        rb[slot, me] = value
        for k in range(1, NS):
            start(None, r_copy(k, slot))

    def reduce_done(slot):
        for k in range(1, NS):
            wait_recv(None, r_copy(k, slot))
        total = rb[slot, 0]
        for k in range(1, NS):
            total = total + rb[slot, k]
        return total

    for d in range(2):
        start(has[d], ini_copy(d, 1))
        start(has[d], ini_copy(d, 0))

    def fold(v):
        return jnp.sum(v.reshape(Z // 8, 8, Y), axis=0)

    cls = tc_ref[0]
    tons = jnp.zeros((Z, Y), jnp.float32)
    for c in range(dens_ref.shape[0]):
        tons = jnp.where(cls == c, (1.0 + c) * dens_ref[c], tons)
    ton[...] = tons
    rows = lax.broadcasted_iota(jnp.int32, (R, Y), 0)
    part = jnp.sum(tons, axis=0, keepdims=True)
    reduce_start(0, jnp.where(rows == 0, part, 0.0))

    z_ids = lax.broadcasted_iota(jnp.int32, (Z, Y), 0)
    y_ids = lax.broadcasted_iota(jnp.int32, (Z, Y), 1)

    def mask_of(codes, k, inside):
        ok = z_ids >= 1
        if k > 0:
            ok = ok & (jnp.broadcast_to((codes >> (k - 1)) & 1, (Z, Y)) == 1)
        if k == 3:
            ok = ok & (y_ids < Y - 1)
        if k == 4:
            ok = ok & (y_ids >= 1)
        if inside is not None:
            ok = ok & (jnp.full((Z, Y), inside.astype(jnp.int32)) == 1)
        return ok.astype(jnp.float32)

    own = slope_ref[...]
    act[0] = mask_of(own, 0, None)
    act[1] = mask_of(own, 1, me < NS - 1)
    act[2] = mask_of(own, 2, me > 0)
    act[3] = mask_of(own, 3, None)
    act[4] = mask_of(own, 4, None)

    period = [(pe * T + t).astype(jnp.float32) for t in range(T)]
    pid = [jnp.full((1, Y), period[t]) for t in range(T)]
    disc = [jnp.exp(-RATE * pid[t]) for t in range(T)]
    tonr = ton[...] * (1.0 / root_blocks)
    for t in range(T):
        tb[t] = 1.0 / (SLOPE * (total_periods - pid[t]) + tonr)
        uf[t] = u_ref[0, t]
        bf[t] = bound_ref[0, t]
        for k in range(5):
            fa[k, t] = prec_ref[k, 0, t] * act[k]

    caps = jnp.zeros((R, Y), jnp.float32)
    climit = jnp.zeros((R, Y), jnp.float32)
    for t in range(T):
        caps = jnp.where(rows == t, cap_ref[t], caps)
        climit = jnp.where(rows == t, capacity_ref[t] * blocks_all, climit)
    w = jnp.full((1, Y), om_ref[0])

    for d in range(2):
        @pl.when(jnp.logical_not(gets[d]))
        def _():
            act[5 + d] = jnp.zeros((Z, Y), jnp.float32)
            fa[5 + d] = jnp.zeros((T, Z, Y), jnp.float32)
            for s in range(STEPS):
                xr[d, s] = jnp.zeros((T, Z, Y), jnp.float32)

        wait_recv(gets[d], ini_copy(d, 1))
        wait_recv(gets[d], ini_copy(d, 0))

        @pl.when(gets[d])
        def _():
            act[5 + d] = mask_of(slr[d], 1 + d, None)
            for t in range(T):
                fa[5 + d, t] = fa[5 + d, t] * act[5 + d]

    def up_y(v):
        return pltpu.roll(v, 1, 1)

    def dn_y(v):
        return pltpu.roll(v, Y - 1, 1)

    def up_z(v):
        return pltpu.roll(v, 1, 0)

    def dn_z(v):
        return pltpu.roll(v, Z - 1, 0)

    def settle(first, cur, acc, at, j, new, old):
        if j == 0:
            cur[at] = new
            return new, None
        if j == 1:
            cur[at] = new
            acc[at] = old + new
            return new, None
        mean = (acc[at] + new) * (1.0 / INNER)
        diff = mean - first[at]
        first[at] = mean
        return mean, fold(diff * diff)

    def gradient(s, arcs, bounds):
        tail = None
        for t in range(T - 1, -1, -1):
            p = [arcs[k, t] for k in range(5)]
            g = (((p[0] + p[1]) + (p[2] + p[3])) + p[4]) + bounds[t]
            back = ((p[0] + arcs[5, t]) + arcs[6, t]) + (up_y(p[3]) + dn_y(p[4]))
            g = g - dn_z(back)
            tail = g if tail is None else tail + g
            tl[t] = tail
        as_[s] = tail
        for k in range(1, NPD):
            start(pe >= k, a_copy(k, s))

    gradient(0, fa, bf)
    tons_all = jnp.sum(jnp.sum(reduce_done(0), axis=0, keepdims=True), axis=1, keepdims=True)
    inv_tons = 1.0 / tons_all
    cap_first = cap_sum = None

    for s in range(STEPS):
        j = s % INNER
        u_src = uf if j == 0 else uc
        b_src = bf if j == 0 else bc
        p_src = fa if j == 0 else ca
        inv_w = 1.0 / w
        move_p = jnp.zeros((8, Y), jnp.float32)
        move_d = jnp.zeros((8, Y), jnp.float32)
        for k in range(1, NPD):
            @pl.when(pe + k < NPD)
            def _():
                a_copy(k, s).wait_recv()
                for t in range(T):
                    tl[t] = tl[t] + ar[s, k - 1]
        head = None
        row = jnp.zeros((R, Y), jnp.float32)
        for t in range(T):
            old = u_src[t]
            grad = tl[t] + (ton[...] * (1.0 / root_blocks)) * caps[t : t + 1, :]
            new = jnp.maximum(old - (tb[t] * inv_w) * (grad - bv_ref[0] * disc[t]), 0.0)
            ext = 2.0 * new - old
            _, moved = settle(uf, uc, us, t, j, new, old)
            if moved is not None:
                move_p = move_p + moved
            if t == 0:
                ex0[...] = ext
            else:
                xs[s, t] = ext
            head = ext if head is None else head + ext
            row = jnp.where(rows == t, jnp.sum(ton[...] * ext, axis=0, keepdims=True), row)
        es[s] = head
        for k in range(1, NPD):
            start(pe + k < NPD, e_copy(k, s))
        for d in range(2):
            start(has[d], x_copy(d, 0, s))
        reduce_start(1 + s, row)
        for k in range(1, NPD):
            @pl.when(pe >= k)
            def _():
                e_copy(k, s).wait_recv()
                ex0[...] = ex0[...] + er[s, k - 1]
        xs[s, 0] = ex0[...]
        for d in range(2):
            start(has[d], x_copy(d, 1, s))
        total = None
        for t in range(T):
            total = xs[s, t] if t == 0 else total + xs[s, t]
            cb[t] = total
        rate_b = [w / (pid[t] + 1.0) for t in range(T)]
        rate_p = [w / (2.0 * (pid[t] + 1.0)) for t in range(T)]

        def arc(k, t, diff, move):
            old = p_src[k, t]
            new = jnp.maximum(old + rate_p[t] * diff, 0.0) * act[k]
            _, moved = settle(fa, ca, sa, (k, t), j, new, old)
            if moved is not None and k < 5:
                move = move + moved
            return move

        for t in range(T):
            c = cb[t]
            old = b_src[t]
            new = jnp.maximum(old + rate_b[t] * (c - 1.0), 0.0)
            _, moved = settle(bf, bc, bs, t, j, new, old)
            if moved is not None:
                move_d = move_d + moved
            cz = up_z(c)
            move_d = arc(0, t, c - cz, move_d)
            move_d = arc(3, t, c - dn_y(cz), move_d)
            move_d = arc(4, t, c - up_y(cz), move_d)
        for part in range(2):
            for d in range(2):
                wait_recv(gets[d], x_copy(d, part, s))
        total_m = total_p = None
        for t in range(T):
            total_m = xr[0, s, t] if t == 0 else total_m + xr[0, s, t]
            total_p = xr[1, s, t] if t == 0 else total_p + xr[1, s, t]
            c = cb[t]
            cz = up_z(c)
            move_d = arc(1, t, c - up_z(total_p), move_d)
            move_d = arc(2, t, c - up_z(total_m), move_d)
            move_d = arc(5, t, total_m - cz, move_d)
            move_d = arc(6, t, total_p - cz, move_d)
        last = j == INNER - 1
        if s < STEPS - 1:
            gradient(s + 1, fa if last else ca, bf if last else bc)
        if last:
            cyc = s // INNER
            mp = jnp.sum(move_p, axis=0, keepdims=True)
            md = jnp.sum(move_d, axis=0, keepdims=True)
            reduce_start(1 + STEPS + cyc, jnp.where(rows == 0, mp, jnp.where(rows == 1, md, 0.0)))
        row_total = jnp.sum(reduce_done(1 + s), axis=1, keepdims=True)
        new_caps = jnp.maximum(caps + w * ((row_total - climit) * inv_tons), 0.0)
        new_caps = jnp.where(rows < T, new_caps, 0.0)
        if j == 0:
            cap_first = caps
            cap_sum = new_caps
        else:
            cap_sum = cap_sum + new_caps
        caps = new_caps
        if last:
            caps = cap_sum * (1.0 / INNER)
            cap_move = jnp.sum((caps - cap_first) ** 2, axis=0, keepdims=True)
            got = jnp.sum(reduce_done(1 + STEPS + cyc), axis=1, keepdims=True)
            msg = jnp.broadcast_to(got, (R, Y)) + jnp.where(rows == 1, cap_move, 0.0)
            ps[cyc] = msg
            pb[cyc, pe] = msg
            for k in range(1, NPD):
                start(None, p_copy(k, cyc))
            if s == STEPS - 1:
                for t in range(T):
                    u_out[0, t] = uf[t]
                    bound_out[0, t] = bf[t]
                    for k in range(5):
                        prec_out[k, 0, t] = fa[k, t]
                    cap_out[t] = caps[t, 0]
            for k in range(1, NPD):
                wait_recv(None, p_copy(k, cyc))
            tot = pb[cyc, 0]
            for k in range(1, NPD):
                tot = tot + pb[cyc, k]
            w = jnp.sqrt(w * jnp.sqrt((tot[1:2, :] + EPS) / (tot[0:1, :] + EPS)))
    w_out[0] = w[0, 0]
    for cond, copy in sends:
        if cond is None:
            copy.wait_send()
        else:
            pl.when(cond)(lambda copy=copy: copy.wait_send())


def solution(mesh):
    NS, NPD = mesh.shape["strip"], mesh.shape["period"]

    def per_device(u, prec, bound, cap, capacity, bv, tc, dens, slope, om):
        rows_here, T, Z, Y = u.shape
        assert rows_here == 1
        R = -(-T // 8) * 8
        f32 = jnp.float32
        vmem = pl.BlockSpec(memory_space=pltpu.VMEM)
        smem = pl.BlockSpec(memory_space=pltpu.SMEM)
        plane = lambda *n: pltpu.VMEM((*n, Z, Y), f32)
        dma = pltpu.SemaphoreType.DMA
        slots = 1 + STEPS + OUTER
        far = max(NPD - 1, 1)
        return pl.pallas_call(
            functools.partial(kernel, NS, NPD, T, Z, Y, R),
            out_shape=(
                jax.ShapeDtypeStruct(u.shape, f32),
                jax.ShapeDtypeStruct(prec.shape, f32),
                jax.ShapeDtypeStruct(bound.shape, f32),
                jax.ShapeDtypeStruct(cap.shape, f32),
                jax.ShapeDtypeStruct((1,), f32),
            ),
            in_specs=[vmem, vmem, vmem, smem, smem, vmem, vmem, smem, vmem, smem],
            out_specs=(vmem, vmem, vmem, smem, smem),
            scratch_shapes=[
                plane(T), plane(T), plane(T), plane(T), plane(T), plane(T),
                plane(7, T), plane(7, T), plane(7, T), plane(7), plane(), plane(T), plane(T), plane(T), plane(),
                plane(STEPS, T), plane(2, STEPS, T), plane(STEPS), plane(STEPS, far),
                plane(STEPS), plane(STEPS, far),
                pltpu.VMEM((slots, R, Y), f32), pltpu.VMEM((slots, NS, R, Y), f32),
                pltpu.VMEM((OUTER, R, Y), f32), pltpu.VMEM((OUTER, NPD, R, Y), f32),
                pltpu.VMEM((2, 1, Y), jnp.int32),
                dma((2, 2)), dma((2, 2)), dma((2, 2, STEPS)), dma((2, 2, STEPS)),
                dma((STEPS, far)), dma((STEPS, far)), dma((STEPS, far)), dma((STEPS, far)),
                dma((slots, NS - 1)), dma((slots, NS - 1)), dma((OUTER, far)), dma((OUTER, far)),
            ],
            compiler_params=pltpu.CompilerParams(collective_id=0, has_side_effects=True),
        )(u, prec, bound, cap, capacity, bv, tc, dens, slope, om)

    in_specs = (
        P("strip", "period", None, None),
        P(None, "strip", "period", None, None),
        P("strip", "period", None, None),
        P("period"),
        P("period"),
        P("strip", None, None),
        P("strip", None, None),
        P(),
        P("strip", None),
        P(),
    )
    out_specs = (
        P("strip", "period", None, None),
        P(None, "strip", "period", None, None),
        P("strip", "period", None, None),
        P("period"),
        P(),
    )
    return jax.shard_map(
        per_device, mesh=mesh, in_specs=in_specs, out_specs=out_specs, check_vma=False
    )
```

```python
import functools
import math

import jax
import jax.numpy as jnp
from jax import lax
from jax.experimental import pallas as pl
from jax.experimental.pallas import tpu as pltpu
from jax.sharding import PartitionSpec as P

OUTER = 2
INNER = 3
STEPS = OUTER * INNER
RATE = math.log(1.1) / 12.0
EPS = 1e-06
SLOPE = 11.0
MESH = pl.DeviceIdType.MESH


def kernel(
    NS, NPD, T, Z, Y, R,
    u_ref, prec_ref, bound_ref, cap_ref, capacity_ref, bv_ref, tc_ref, dens_ref, slope_ref, om_ref,
    u_out, prec_out, bound_out, cap_out, w_out,
    uf, uc, us, bf, bc, bs, fa, ca, sa, act, ton, tb, tl, cb, ex0,
    xs, xr, es, er, as_, ar, rs, rb, ps, pb, slr,
    praw, ti, to_sum, loc, ini_s, ini_r, xs_s, xs_r, e_s, e_r, a_s, a_r, r_s, r_r, p_s, p_r,
):
    me = lax.axis_index("strip")
    pe = lax.axis_index("period")
    total_rows = NS
    total_periods = NPD * T
    blocks_all = float(total_rows * Z * Y)
    root_blocks = math.sqrt(blocks_all)
    sends = []

    loads = (
        pltpu.make_async_copy(prec_ref.at[:, 0], praw, loc.at[0]),
        pltpu.make_async_copy(bound_ref.at[0], bf, loc.at[1]),
        pltpu.make_async_copy(u_ref.at[0], uf, loc.at[2]),
    )
    for load in loads:
        load.start()
    barrier = pltpu.get_barrier_semaphore()
    for k in range(1, NS):
        pl.semaphore_signal(barrier, inc=1, device_id={"strip": lax.rem(me + k, NS)}, device_id_type=MESH)
    for k in range(1, NPD):
        pl.semaphore_signal(barrier, inc=1, device_id={"period": lax.rem(pe + k, NPD)}, device_id_type=MESH)

    has = (me < NS - 1, me > 0)
    gets = (me > 0, me < NS - 1)
    to = (me + 1, me - 1)

    def remote(src, dst, ss, rr, dev):
        return pltpu.make_async_remote_copy(
            src_ref=src, dst_ref=dst, send_sem=ss, recv_sem=rr, device_id=dev, device_id_type=MESH
        )

    def ini_copy(d, what):
        if what == 2:
            return remote(to_sum.at[d], ti.at[d], ini_s.at[d, 2], ini_r.at[d, 2], {"strip": to[d]})
        if what == 0:
            rest = pl.ds(1, T - 1)
            return remote(praw.at[1 + d, rest], fa.at[5 + d, rest], ini_s.at[d, 0], ini_r.at[d, 0], {"strip": to[d]})
        return remote(slope_ref, slr.at[d], ini_s.at[d, 1], ini_r.at[d, 1], {"strip": to[d]})

    def x_copy(d, part, s):
        lo, size = (1, T - 1) if part == 0 else (0, 1)
        return remote(
            xs.at[s, pl.ds(lo, size)], xr.at[d, s, pl.ds(lo, size)],
            xs_s.at[d, part, s], xs_r.at[d, part, s], {"strip": to[d]},
        )

    def e_copy(k, s):
        return remote(es.at[s], er.at[s, k - 1], e_s.at[s, k - 1], e_r.at[s, k - 1], {"period": pe + k})

    def a_copy(k, s):
        return remote(as_.at[s], ar.at[s, k - 1], a_s.at[s, k - 1], a_r.at[s, k - 1], {"period": pe - k})

    def r_copy(k, slot):
        return remote(
            rs.at[slot], rb.at[slot, me], r_s.at[slot, k - 1], r_r.at[slot, k - 1],
            {"strip": lax.rem(me + k, NS)},
        )

    def p_copy(k, slot):
        return remote(
            ps.at[slot], pb.at[slot, pe], p_s.at[slot, k - 1], p_r.at[slot, k - 1],
            {"period": lax.rem(pe + k, NPD)},
        )

    def start(cond, copy):
        def go():
            copy.start()
        if cond is None:
            go()
        else:
            pl.when(cond)(go)
        sends.append((cond, copy))

    def wait_recv(cond, copy):
        if cond is None:
            copy.wait_recv()
        else:
            pl.when(cond)(lambda: copy.wait_recv())

    def reduce_start(slot, value):
        rs[slot] = value
        rb[slot, me] = value
        for k in range(1, NS):
            start(None, r_copy(k, slot))

    def reduce_done(slot):
        for k in range(1, NS):
            wait_recv(None, r_copy(k, slot))
        total = rb[slot, 0]
        for k in range(1, NS):
            total = total + rb[slot, k]
        return total

    loads[0].wait()
    for d in range(2):
        total = praw[1 + d, 0]
        for t in range(1, T):
            total = total + praw[1 + d, t]
        to_sum[d] = total
    pl.semaphore_wait(barrier, NS + NPD - 2)
    for d in range(2):
        start(has[d], ini_copy(d, 1))
        start(has[d], ini_copy(d, 2))
    for d in range(2):
        start(has[d], ini_copy(d, 0))

    rows = lax.broadcasted_iota(jnp.int32, (R, Y), 0)
    lanes = lax.broadcasted_iota(jnp.int32, (R, Y), 1)

    def as_lanes(value):
        sums = jnp.sum(value, axis=1, keepdims=True)
        return jnp.sum(jnp.where(lanes == rows, sums, 0.0), axis=0, keepdims=True)

    def as_rows(line):
        return jnp.sum(jnp.where(lanes == rows, line, 0.0), axis=1, keepdims=True)

    def fold(v):
        return jnp.sum(v.reshape(Z // 8, 8, Y), axis=0)

    cls = tc_ref[0]
    tons = jnp.zeros((Z, Y), jnp.float32)
    for c in range(dens_ref.shape[0]):
        tons = jnp.where(cls == c, (1.0 + c) * dens_ref[c], tons)
    ton[...] = tons
    part = jnp.sum(tons, axis=0, keepdims=True)
    reduce_start(0, part)

    z_ids = lax.broadcasted_iota(jnp.int32, (Z, Y), 0)
    y_ids = lax.broadcasted_iota(jnp.int32, (Z, Y), 1)

    def mask_of(codes, k, inside):
        ok = z_ids >= 1
        if k > 0:
            ok = ok & (jnp.broadcast_to((codes >> (k - 1)) & 1, (Z, Y)) == 1)
        if k == 3:
            ok = ok & (y_ids < Y - 1)
        if k == 4:
            ok = ok & (y_ids >= 1)
        if inside is not None:
            ok = ok & (jnp.full((Z, Y), inside.astype(jnp.int32)) == 1)
        return ok.astype(jnp.float32)

    own = slope_ref[...]
    act[0] = mask_of(own, 0, None)
    act[1] = mask_of(own, 1, me < NS - 1)
    act[2] = mask_of(own, 2, me > 0)
    act[3] = mask_of(own, 3, None)
    act[4] = mask_of(own, 4, None)

    period = [(pe * T + t).astype(jnp.float32) for t in range(T)]
    pid = [jnp.full((1, Y), period[t]) for t in range(T)]
    disc = [jnp.exp(-RATE * pid[t]) for t in range(T)]
    tonr = ton[...] * (1.0 / root_blocks)
    for load in loads[1:]:
        load.wait()
    for t in range(T):
        tb[t] = 1.0 / (SLOPE * (total_periods - pid[t]) + tonr)
        for k in range(5):
            fa[k, t] = praw[k, t] * act[k]

    caps = jnp.zeros((R, Y), jnp.float32)
    climit = jnp.zeros((R, Y), jnp.float32)
    for t in range(T):
        caps = jnp.where(rows == t, cap_ref[t], caps)
        climit = jnp.where(rows == t, capacity_ref[t] * blocks_all, climit)
    w = jnp.full((1, Y), om_ref[0])

    for d in range(2):
        @pl.when(jnp.logical_not(gets[d]))
        def _():
            act[5 + d] = jnp.zeros((Z, Y), jnp.float32)
            ti[d] = jnp.zeros((Z, Y), jnp.float32)
            fa[5 + d] = jnp.zeros((T, Z, Y), jnp.float32)
            for s in range(STEPS):
                xr[d, s] = jnp.zeros((T, Z, Y), jnp.float32)

    def up_y(v):
        return pltpu.roll(v, 1, 1)

    def dn_y(v):
        return pltpu.roll(v, Y - 1, 1)

    def up_z(v):
        return pltpu.roll(v, 1, 0)

    def dn_z(v):
        return pltpu.roll(v, Z - 1, 0)

    def settle(first, cur, acc, at, j, new, old):
        if j == 0:
            cur[at] = new
            return new, None
        if j == 1:
            cur[at] = new
            acc[at] = old + new
            return new, None
        mean = (acc[at] + new) * (1.0 / INNER)
        diff = mean - first[at]
        first[at] = mean
        return mean, fold(diff * diff)

    def gradient(s, arcs, bounds):
        tail = None
        for t in range(T - 1, -1, -1):
            p = [arcs[k, t] for k in range(5)]
            g = (((p[0] + p[1]) + (p[2] + p[3])) + p[4]) + bounds[t]
            back = ((p[0] + arcs[5, t]) + arcs[6, t]) + (up_y(p[3]) + dn_y(p[4]))
            g = g - dn_z(back)
            tail = g if tail is None else tail + g
            tl[t] = tail
        as_[s] = tail
        for k in range(1, NPD):
            start(pe >= k, a_copy(k, s))

    tail = None
    for t in range(T - 1, -1, -1):
        p = [fa[k, t] for k in range(5)]
        g = (((p[0] + p[1]) + (p[2] + p[3])) + p[4]) + bf[t]
        g = g - dn_z(p[0] + (up_y(p[3]) + dn_y(p[4])))
        tail = g if tail is None else tail + g
        tl[t] = tail
    for d in range(2):
        wait_recv(gets[d], ini_copy(d, 1))
        wait_recv(gets[d], ini_copy(d, 2))

        @pl.when(gets[d])
        def _():
            act[5 + d] = mask_of(slr[d], 1 + d, None)
    as_[0] = tl[0] - dn_z(ti[0] * act[5] + ti[1] * act[6])
    for k in range(1, NPD):
        start(pe >= k, a_copy(k, 0))
    for d in range(2):
        wait_recv(gets[d], ini_copy(d, 0))
        rest = ti[d]
        for t in range(1, T):
            plane = fa[5 + d, t]
            rest = rest - plane
            fa[5 + d, t] = plane * act[5 + d]
        fa[5 + d, 0] = rest * act[5 + d]
    tail = None
    for t in range(T - 1, -1, -1):
        back = fa[5, t] + fa[6, t]
        tail = back if tail is None else tail + back
        tl[t] = tl[t] - dn_z(tail)
    tons_all = jnp.sum(reduce_done(0), axis=1, keepdims=True)
    inv_tons = 1.0 / tons_all
    cap_first = cap_sum = None

    for s in range(STEPS):
        j = s % INNER
        u_src = uf if j == 0 else uc
        b_src = bf if j == 0 else bc
        p_src = fa if j == 0 else ca
        inv_w = 1.0 / w
        move_p = jnp.zeros((8, Y), jnp.float32)
        move_d = jnp.zeros((8, Y), jnp.float32)
        for k in range(1, NPD):
            @pl.when(pe + k < NPD)
            def _():
                a_copy(k, s).wait_recv()
                for t in range(T):
                    tl[t] = tl[t] + ar[s, k - 1]
        head = None
        row = jnp.zeros((R, Y), jnp.float32)
        for t in range(T):
            old = u_src[t]
            grad = tl[t] + (ton[...] * (1.0 / root_blocks)) * caps[t : t + 1, :]
            new = jnp.maximum(old - (tb[t] * inv_w) * (grad - bv_ref[0] * disc[t]), 0.0)
            ext = 2.0 * new - old
            _, moved = settle(uf, uc, us, t, j, new, old)
            if moved is not None:
                move_p = move_p + moved
            if t == 0:
                ex0[...] = ext
            else:
                xs[s, t] = ext
            head = ext if head is None else head + ext
            row = jnp.where(rows == t, jnp.sum(ton[...] * ext, axis=0, keepdims=True), row)
        es[s] = head
        for k in range(1, NPD):
            start(pe + k < NPD, e_copy(k, s))
        for d in range(2):
            start(has[d], x_copy(d, 0, s))
        reduce_start(1 + s, as_lanes(row))
        for k in range(1, NPD):
            @pl.when(pe >= k)
            def _():
                e_copy(k, s).wait_recv()
                ex0[...] = ex0[...] + er[s, k - 1]
        xs[s, 0] = ex0[...]
        for d in range(2):
            start(has[d], x_copy(d, 1, s))
        total = None
        for t in range(T):
            total = xs[s, t] if t == 0 else total + xs[s, t]
            cb[t] = total
        rate_b = [w / (pid[t] + 1.0) for t in range(T)]
        rate_p = [w / (2.0 * (pid[t] + 1.0)) for t in range(T)]

        def arc(k, t, diff, move):
            old = p_src[k, t]
            new = jnp.maximum(old + rate_p[t] * diff, 0.0) * act[k]
            _, moved = settle(fa, ca, sa, (k, t), j, new, old)
            if moved is not None and k < 5:
                move = move + moved
            return move

        for t in range(T):
            c = cb[t]
            old = b_src[t]
            new = jnp.maximum(old + rate_b[t] * (c - 1.0), 0.0)
            _, moved = settle(bf, bc, bs, t, j, new, old)
            if moved is not None:
                move_d = move_d + moved
            cz = up_z(c)
            move_d = arc(0, t, c - cz, move_d)
            move_d = arc(3, t, c - dn_y(cz), move_d)
            move_d = arc(4, t, c - up_y(cz), move_d)
        for part in range(2):
            for d in range(2):
                wait_recv(gets[d], x_copy(d, part, s))
        total_m = total_p = None
        for t in range(T):
            total_m = xr[0, s, t] if t == 0 else total_m + xr[0, s, t]
            total_p = xr[1, s, t] if t == 0 else total_p + xr[1, s, t]
            c = cb[t]
            cz = up_z(c)
            move_d = arc(1, t, c - up_z(total_p), move_d)
            move_d = arc(2, t, c - up_z(total_m), move_d)
            move_d = arc(5, t, total_m - cz, move_d)
            move_d = arc(6, t, total_p - cz, move_d)
        last = j == INNER - 1
        if s < STEPS - 1:
            gradient(s + 1, fa if last else ca, bf if last else bc)
        if last:
            cyc = s // INNER
            mp = jnp.sum(move_p, axis=0, keepdims=True)
            md = jnp.sum(move_d, axis=0, keepdims=True)
            reduce_start(1 + STEPS + cyc, as_lanes(jnp.where(rows == 0, mp, jnp.where(rows == 1, md, 0.0))))
        row_total = as_rows(reduce_done(1 + s))
        new_caps = jnp.maximum(caps + w * ((row_total - climit) * inv_tons), 0.0)
        new_caps = jnp.where(rows < T, new_caps, 0.0)
        if j == 0:
            cap_first = caps
            cap_sum = new_caps
        else:
            cap_sum = cap_sum + new_caps
        caps = new_caps
        if last:
            caps = cap_sum * (1.0 / INNER)
            cap_move = jnp.sum((caps - cap_first) ** 2, axis=0, keepdims=True)
            got = reduce_done(1 + STEPS + cyc)
            msg = got + jnp.where(lanes[0:1] == 1, cap_move, 0.0)
            ps[cyc] = msg
            pb[cyc, pe] = msg
            for k in range(1, NPD):
                start(None, p_copy(k, cyc))
            if s == STEPS - 1:
                for t in range(T):
                    u_out[0, t] = uf[t]
                    bound_out[0, t] = bf[t]
                    for k in range(5):
                        prec_out[k, 0, t] = fa[k, t]
                    cap_out[t] = caps[t, 0]
            for k in range(1, NPD):
                wait_recv(None, p_copy(k, cyc))
            tot = pb[cyc, 0]
            for k in range(1, NPD):
                tot = tot + pb[cyc, k]
            tot = as_rows(tot)
            moved = jnp.sqrt((tot[1:2, :] + EPS) / (tot[0:1, :] + EPS))
            w = jnp.sqrt(w * moved)
    w_out[0] = w[0, 0]
    for cond, copy in sends:
        if cond is None:
            copy.wait_send()
        else:
            pl.when(cond)(lambda copy=copy: copy.wait_send())


def solution(mesh):
    NS, NPD = mesh.shape["strip"], mesh.shape["period"]

    def per_device(u, prec, bound, cap, capacity, bv, tc, dens, slope, om):
        rows_here, T, Z, Y = u.shape
        assert rows_here == 1
        R = -(-T // 8) * 8
        f32 = jnp.float32
        vmem = pl.BlockSpec(memory_space=pltpu.VMEM)
        hbm = pl.BlockSpec(memory_space=pl.ANY)
        smem = pl.BlockSpec(memory_space=pltpu.SMEM)
        plane = lambda *n: pltpu.VMEM((*n, Z, Y), f32)
        dma = pltpu.SemaphoreType.DMA
        slots = 1 + STEPS + OUTER
        far = max(NPD - 1, 1)
        return pl.pallas_call(
            functools.partial(kernel, NS, NPD, T, Z, Y, R),
            out_shape=(
                jax.ShapeDtypeStruct(u.shape, f32),
                jax.ShapeDtypeStruct(prec.shape, f32),
                jax.ShapeDtypeStruct(bound.shape, f32),
                jax.ShapeDtypeStruct(cap.shape, f32),
                jax.ShapeDtypeStruct((1,), f32),
            ),
            in_specs=[hbm, hbm, hbm, smem, smem, vmem, vmem, smem, vmem, smem],
            out_specs=(vmem, vmem, vmem, smem, smem),
            scratch_shapes=[
                plane(T), plane(T), plane(T), plane(T), plane(T), plane(T),
                plane(7, T), plane(7, T), plane(7, T), plane(7), plane(), plane(T), plane(T), plane(T), plane(),
                plane(STEPS, T), plane(2, STEPS, T), plane(STEPS), plane(STEPS, far),
                plane(STEPS), plane(STEPS, far),
                pltpu.VMEM((slots, 1, Y), f32), pltpu.VMEM((slots, NS, 1, Y), f32),
                pltpu.VMEM((OUTER, 1, Y), f32), pltpu.VMEM((OUTER, NPD, 1, Y), f32),
                pltpu.VMEM((2, 1, Y), jnp.int32),
                plane(5, T), plane(2), plane(2), dma((3,)),
                dma((2, 3)), dma((2, 3)), dma((2, 2, STEPS)), dma((2, 2, STEPS)),
                dma((STEPS, far)), dma((STEPS, far)), dma((STEPS, far)), dma((STEPS, far)),
                dma((slots, NS - 1)), dma((slots, NS - 1)), dma((OUTER, far)), dma((OUTER, far)),
            ],
            compiler_params=pltpu.CompilerParams(collective_id=0, has_side_effects=True),
        )(u, prec, bound, cap, capacity, bv, tc, dens, slope, om)

    in_specs = (
        P("strip", "period", None, None),
        P(None, "strip", "period", None, None),
        P("strip", "period", None, None),
        P("period"),
        P("period"),
        P("strip", None, None),
        P("strip", None, None),
        P(),
        P("strip", None),
        P(),
    )
    out_specs = (
        P("strip", "period", None, None),
        P(None, "strip", "period", None, None),
        P("strip", "period", None, None),
        P("period"),
        P(),
    )
    return jax.shard_map(
        per_device, mesh=mesh, in_specs=in_specs, out_specs=out_specs, check_vma=False
    )
```

```python
import functools
import math

import jax
import jax.numpy as jnp
from jax import lax
from jax.experimental import pallas as pl
from jax.experimental.pallas import tpu as pltpu
from jax.sharding import PartitionSpec as P

OUTER = 2
INNER = 3
STEPS = OUTER * INNER
RATE = math.log(1.1) / 12.0
EPS = 1e-06
SLOPE = 11.0
MESH = pl.DeviceIdType.MESH


def kernel(
    NS, NPD, T, Z, Y, R,
    u_ref, prec_ref, bound_ref, cap_ref, capacity_ref, bv_ref, tc_ref, dens_ref, slope_ref, om_ref,
    u_out, prec_out, bound_out, cap_out, w_out,
    uf, uc, us, bf, bc, bs, fa, ca, sa, act, ton, tb, tl, cb, ex0,
    xs, xr, es, er, as_, ar, rs, rb, ps, pb, slr,
    praw, ti, to_sum, loc, ini_s, ini_r, xs_s, xs_r, e_s, e_r, a_s, a_r, r_s, r_r, p_s, p_r,
):
    me = lax.axis_index("strip")
    pe = lax.axis_index("period")
    total_rows = NS
    total_periods = NPD * T
    blocks_all = float(total_rows * Z * Y)
    root_blocks = math.sqrt(blocks_all)
    sends = []

    loads = (
        pltpu.make_async_copy(prec_ref.at[:, 0], praw, loc.at[0]),
        pltpu.make_async_copy(bound_ref.at[0], bf, loc.at[1]),
        pltpu.make_async_copy(u_ref.at[0], uf, loc.at[2]),
    )
    for load in loads:
        load.start()
    barrier = pltpu.get_barrier_semaphore()
    for k in range(1, NS):
        pl.semaphore_signal(barrier, inc=1, device_id={"strip": lax.rem(me + k, NS)}, device_id_type=MESH)
    for k in range(1, NPD):
        pl.semaphore_signal(barrier, inc=1, device_id={"period": lax.rem(pe + k, NPD)}, device_id_type=MESH)

    has = (me < NS - 1, me > 0)
    gets = (me > 0, me < NS - 1)
    to = (me + 1, me - 1)

    def remote(src, dst, ss, rr, dev):
        return pltpu.make_async_remote_copy(
            src_ref=src, dst_ref=dst, send_sem=ss, recv_sem=rr, device_id=dev, device_id_type=MESH
        )

    def ini_copy(d, what):
        if what == 2:
            return remote(to_sum.at[d], ti.at[d], ini_s.at[d, 2], ini_r.at[d, 2], {"strip": to[d]})
        if what == 0:
            rest = pl.ds(1, T - 1)
            return remote(praw.at[1 + d, rest], fa.at[5 + d, rest], ini_s.at[d, 0], ini_r.at[d, 0], {"strip": to[d]})
        return remote(slope_ref, slr.at[d], ini_s.at[d, 1], ini_r.at[d, 1], {"strip": to[d]})

    def x_copy(d, part, s):
        lo, size = (1, T - 1) if part == 0 else (0, 1)
        return remote(
            xs.at[s, pl.ds(lo, size)], xr.at[d, s, pl.ds(lo, size)],
            xs_s.at[d, part, s], xs_r.at[d, part, s], {"strip": to[d]},
        )

    def e_copy(k, s):
        return remote(es.at[s], er.at[s, k - 1], e_s.at[s, k - 1], e_r.at[s, k - 1], {"period": pe + k})

    def a_copy(k, s):
        return remote(as_.at[s], ar.at[s, k - 1], a_s.at[s, k - 1], a_r.at[s, k - 1], {"period": pe - k})

    def r_copy(k, slot):
        return remote(
            rs.at[slot], rb.at[slot, me], r_s.at[slot, k - 1], r_r.at[slot, k - 1],
            {"strip": lax.rem(me + k, NS)},
        )

    def p_copy(k, slot):
        return remote(
            ps.at[slot], pb.at[slot, pe], p_s.at[slot, k - 1], p_r.at[slot, k - 1],
            {"period": lax.rem(pe + k, NPD)},
        )

    def start(cond, copy):
        def go():
            copy.start()
        if cond is None:
            go()
        else:
            pl.when(cond)(go)
        sends.append((cond, copy))

    def wait_recv(cond, copy):
        if cond is None:
            copy.wait_recv()
        else:
            pl.when(cond)(lambda: copy.wait_recv())

    def reduce_start(slot, value):
        rs[slot] = value
        rb[slot, me] = value
        for k in range(1, NS):
            start(None, r_copy(k, slot))

    def reduce_done(slot):
        for k in range(1, NS):
            wait_recv(None, r_copy(k, slot))
        total = rb[slot, 0]
        for k in range(1, NS):
            total = total + rb[slot, k]
        return total

    loads[0].wait()
    for d in range(2):
        total = praw[1 + d, 0]
        for t in range(1, T):
            total = total + praw[1 + d, t]
        to_sum[d] = total
    pl.semaphore_wait(barrier, NS + NPD - 2)
    for d in range(2):
        start(has[d], ini_copy(d, 1))
        start(has[d], ini_copy(d, 2))
    for d in range(2):
        start(has[d], ini_copy(d, 0))

    rows = lax.broadcasted_iota(jnp.int32, (R, Y), 0)
    lanes = lax.broadcasted_iota(jnp.int32, (R, Y), 1)

    def as_lanes(value):
        sums = jnp.sum(value, axis=1, keepdims=True)
        return jnp.sum(jnp.where(lanes == rows, sums, 0.0), axis=0, keepdims=True)

    def as_rows(line):
        return jnp.sum(jnp.where(lanes == rows, line, 0.0), axis=1, keepdims=True)

    def fold(v):
        return jnp.sum(v.reshape(Z // 8, 8, Y), axis=0)

    cls = tc_ref[0]
    tons = jnp.zeros((Z, Y), jnp.float32)
    for c in range(dens_ref.shape[0]):
        tons = jnp.where(cls == c, (1.0 + c) * dens_ref[c], tons)
    ton[...] = tons
    part = jnp.sum(tons, axis=0, keepdims=True)
    reduce_start(0, part)

    z_ids = lax.broadcasted_iota(jnp.int32, (Z, Y), 0)
    y_ids = lax.broadcasted_iota(jnp.int32, (Z, Y), 1)

    def mask_of(codes, k, inside):
        ok = z_ids >= 1
        if k > 0:
            ok = ok & (jnp.broadcast_to((codes >> (k - 1)) & 1, (Z, Y)) == 1)
        if k == 3:
            ok = ok & (y_ids < Y - 1)
        if k == 4:
            ok = ok & (y_ids >= 1)
        if inside is not None:
            ok = ok & (jnp.full((Z, Y), inside.astype(jnp.int32)) == 1)
        return ok.astype(jnp.float32)

    own = slope_ref[...]
    act[0] = mask_of(own, 0, None)
    act[1] = mask_of(own, 1, me < NS - 1)
    act[2] = mask_of(own, 2, me > 0)
    act[3] = mask_of(own, 3, None)
    act[4] = mask_of(own, 4, None)

    period = [(pe * T + t).astype(jnp.float32) for t in range(T)]
    pid = [jnp.full((1, Y), period[t]) for t in range(T)]
    disc = [jnp.exp(-RATE * pid[t]) for t in range(T)]
    tonr = ton[...] * (1.0 / root_blocks)
    for load in loads[1:]:
        load.wait()
    for t in range(T):
        tb[t] = 1.0 / (SLOPE * (total_periods - pid[t]) + tonr)
        for k in range(5):
            fa[k, t] = praw[k, t] * act[k]

    caps = jnp.zeros((R, Y), jnp.float32)
    climit = jnp.zeros((R, Y), jnp.float32)
    for t in range(T):
        caps = jnp.where(rows == t, cap_ref[t], caps)
        climit = jnp.where(rows == t, capacity_ref[t] * blocks_all, climit)
    w = jnp.full((1, Y), om_ref[0])

    for d in range(2):
        @pl.when(jnp.logical_not(gets[d]))
        def _():
            act[5 + d] = jnp.zeros((Z, Y), jnp.float32)
            ti[d] = jnp.zeros((Z, Y), jnp.float32)
            fa[5 + d] = jnp.zeros((T, Z, Y), jnp.float32)
            for s in range(STEPS):
                xr[d, s] = jnp.zeros((T, Z, Y), jnp.float32)

    def up_y(v):
        return pltpu.roll(v, 1, 1)

    def dn_y(v):
        return pltpu.roll(v, Y - 1, 1)

    def up_z(v):
        return pltpu.roll(v, 1, 0)

    def dn_z(v):
        return pltpu.roll(v, Z - 1, 0)

    def settle(first, cur, acc, at, j, new, old):
        if j == 0:
            cur[at] = new
            return new, None
        if j == 1:
            cur[at] = new
            acc[at] = old + new
            return new, None
        mean = (acc[at] + new) * (1.0 / INNER)
        diff = mean - first[at]
        first[at] = mean
        return mean, fold(diff * diff)

    def gradient_own(arcs, bounds):
        for t in range(T):
            p0, p3, p4 = arcs[0, t], arcs[3, t], arcs[4, t]
            back = p0 + (up_y(p3) + dn_y(p4))
            tl[t] = ((p0 + p3) + (p4 + bounds[t])) - dn_z(back)

    def gradient(s, arcs):
        tail = None
        for t in range(T - 1, -1, -1):
            g = (tl[t] + (arcs[1, t] + arcs[2, t])) - dn_z(arcs[5, t] + arcs[6, t])
            tail = g if tail is None else tail + g
            tl[t] = tail
        as_[s] = tail
        for k in range(1, NPD):
            start(pe >= k, a_copy(k, s))

    tail = None
    for t in range(T - 1, -1, -1):
        p = [fa[k, t] for k in range(5)]
        g = (((p[0] + p[1]) + (p[2] + p[3])) + p[4]) + bf[t]
        g = g - dn_z(p[0] + (up_y(p[3]) + dn_y(p[4])))
        tail = g if tail is None else tail + g
        tl[t] = tail
    for d in range(2):
        wait_recv(gets[d], ini_copy(d, 1))
        wait_recv(gets[d], ini_copy(d, 2))

        @pl.when(gets[d])
        def _():
            act[5 + d] = mask_of(slr[d], 1 + d, None)
    as_[0] = tl[0] - dn_z(ti[0] * act[5] + ti[1] * act[6])
    for k in range(1, NPD):
        start(pe >= k, a_copy(k, 0))
    for d in range(2):
        wait_recv(gets[d], ini_copy(d, 0))
        rest = ti[d]
        for t in range(1, T):
            plane = fa[5 + d, t]
            rest = rest - plane
            fa[5 + d, t] = plane * act[5 + d]
        fa[5 + d, 0] = rest * act[5 + d]
    tail = None
    for t in range(T - 1, -1, -1):
        back = fa[5, t] + fa[6, t]
        tail = back if tail is None else tail + back
        tl[t] = tl[t] - dn_z(tail)
    tons_all = jnp.sum(reduce_done(0), axis=1, keepdims=True)
    inv_tons = 1.0 / tons_all
    cap_first = cap_sum = None

    for s in range(STEPS):
        j = s % INNER
        u_src = uf if j == 0 else uc
        b_src = bf if j == 0 else bc
        p_src = fa if j == 0 else ca
        inv_w = 1.0 / w
        move_p = jnp.zeros((8, Y), jnp.float32)
        move_d = jnp.zeros((8, Y), jnp.float32)
        for k in range(1, NPD):
            @pl.when(pe + k < NPD)
            def _():
                a_copy(k, s).wait_recv()
                for t in range(T):
                    tl[t] = tl[t] + ar[s, k - 1]
        head = None
        row = jnp.zeros((R, Y), jnp.float32)
        for t in range(T):
            old = u_src[t]
            grad = tl[t] + (ton[...] * (1.0 / root_blocks)) * caps[t : t + 1, :]
            new = jnp.maximum(old - (tb[t] * inv_w) * (grad - bv_ref[0] * disc[t]), 0.0)
            ext = 2.0 * new - old
            _, moved = settle(uf, uc, us, t, j, new, old)
            if moved is not None:
                move_p = move_p + moved
            if t == 0:
                ex0[...] = ext
            else:
                xs[s, t] = ext
            head = ext if head is None else head + ext
            row = jnp.where(rows == t, jnp.sum(ton[...] * ext, axis=0, keepdims=True), row)
        es[s] = head
        for k in range(1, NPD):
            start(pe + k < NPD, e_copy(k, s))
        for d in range(2):
            start(has[d], x_copy(d, 0, s))
        for k in range(1, NPD):
            @pl.when(pe >= k)
            def _():
                e_copy(k, s).wait_recv()
                ex0[...] = ex0[...] + er[s, k - 1]
        xs[s, 0] = ex0[...]
        for d in range(2):
            start(has[d], x_copy(d, 1, s))
        reduce_start(1 + s, as_lanes(row))
        total = None
        for t in range(T):
            total = xs[s, t] if t == 0 else total + xs[s, t]
            cb[t] = total
        rate_b = [w / (pid[t] + 1.0) for t in range(T)]
        rate_p = [w / (2.0 * (pid[t] + 1.0)) for t in range(T)]

        def arc(k, t, diff, move):
            old = p_src[k, t]
            new = jnp.maximum(old + rate_p[t] * diff, 0.0) * act[k]
            _, moved = settle(fa, ca, sa, (k, t), j, new, old)
            if moved is not None and k < 5:
                move = move + moved
            return move

        for t in range(T):
            c = cb[t]
            old = b_src[t]
            new = jnp.maximum(old + rate_b[t] * (c - 1.0), 0.0)
            _, moved = settle(bf, bc, bs, t, j, new, old)
            if moved is not None:
                move_d = move_d + moved
            cz = up_z(c)
            move_d = arc(0, t, c - cz, move_d)
            move_d = arc(3, t, c - dn_y(cz), move_d)
            move_d = arc(4, t, c - up_y(cz), move_d)
        last = j == INNER - 1
        if s < STEPS - 1:
            gradient_own(fa if last else ca, bf if last else bc)
        for part in range(2):
            for d in range(2):
                wait_recv(gets[d], x_copy(d, part, s))
        total_m = total_p = None
        for t in range(T):
            total_m = xr[0, s, t] if t == 0 else total_m + xr[0, s, t]
            total_p = xr[1, s, t] if t == 0 else total_p + xr[1, s, t]
            c = cb[t]
            cz = up_z(c)
            move_d = arc(1, t, c - up_z(total_p), move_d)
            move_d = arc(2, t, c - up_z(total_m), move_d)
            if s < STEPS - 1:
                arc(5, t, total_m - cz, None)
                arc(6, t, total_p - cz, None)
        if s < STEPS - 1:
            gradient(s + 1, fa if last else ca)
        if last:
            cyc = s // INNER
            mp = jnp.sum(move_p, axis=0, keepdims=True)
            md = jnp.sum(move_d, axis=0, keepdims=True)
            reduce_start(1 + STEPS + cyc, as_lanes(jnp.where(rows == 0, mp, jnp.where(rows == 1, md, 0.0))))
        row_total = as_rows(reduce_done(1 + s))
        new_caps = jnp.maximum(caps + w * ((row_total - climit) * inv_tons), 0.0)
        new_caps = jnp.where(rows < T, new_caps, 0.0)
        if j == 0:
            cap_first = caps
            cap_sum = new_caps
        else:
            cap_sum = cap_sum + new_caps
        caps = new_caps
        if last:
            caps = cap_sum * (1.0 / INNER)
            cap_move = jnp.sum((caps - cap_first) ** 2, axis=0, keepdims=True)
            got = reduce_done(1 + STEPS + cyc)
            msg = got + jnp.where(lanes[0:1] == 1, cap_move, 0.0)
            ps[cyc] = msg
            pb[cyc, pe] = msg
            for k in range(1, NPD):
                start(None, p_copy(k, cyc))
            if s == STEPS - 1:
                for t in range(T):
                    u_out[0, t] = uf[t]
                    bound_out[0, t] = bf[t]
                    for k in range(5):
                        prec_out[k, 0, t] = fa[k, t]
                    cap_out[t] = caps[t, 0]
            for k in range(1, NPD):
                wait_recv(None, p_copy(k, cyc))
            tot = pb[cyc, 0]
            for k in range(1, NPD):
                tot = tot + pb[cyc, k]
            tot = as_rows(tot)
            moved = jnp.sqrt((tot[1:2, :] + EPS) / (tot[0:1, :] + EPS))
            w = jnp.sqrt(w * moved)
    w_out[0] = w[0, 0]
    for cond, copy in sends:
        if cond is None:
            copy.wait_send()
        else:
            pl.when(cond)(lambda copy=copy: copy.wait_send())


def solution(mesh):
    NS, NPD = mesh.shape["strip"], mesh.shape["period"]

    def per_device(u, prec, bound, cap, capacity, bv, tc, dens, slope, om):
        rows_here, T, Z, Y = u.shape
        assert rows_here == 1
        R = -(-T // 8) * 8
        f32 = jnp.float32
        vmem = pl.BlockSpec(memory_space=pltpu.VMEM)
        hbm = pl.BlockSpec(memory_space=pl.ANY)
        smem = pl.BlockSpec(memory_space=pltpu.SMEM)
        plane = lambda *n: pltpu.VMEM((*n, Z, Y), f32)
        dma = pltpu.SemaphoreType.DMA
        slots = 1 + STEPS + OUTER
        far = max(NPD - 1, 1)
        return pl.pallas_call(
            functools.partial(kernel, NS, NPD, T, Z, Y, R),
            out_shape=(
                pltpu.VMEM(u.shape, f32),
                pltpu.VMEM(prec.shape, f32),
                pltpu.VMEM(bound.shape, f32),
                jax.ShapeDtypeStruct(cap.shape, f32),
                jax.ShapeDtypeStruct((1,), f32),
            ),
            in_specs=[hbm, hbm, hbm, smem, smem, vmem, vmem, smem, vmem, smem],
            out_specs=(vmem, vmem, vmem, smem, smem),
            scratch_shapes=[
                plane(T), plane(T), plane(T), plane(T), plane(T), plane(T),
                plane(7, T), plane(7, T), plane(7, T), plane(7), plane(), plane(T), plane(T), plane(T), plane(),
                plane(STEPS, T), plane(2, STEPS, T), plane(STEPS), plane(STEPS, far),
                plane(STEPS), plane(STEPS, far),
                pltpu.VMEM((slots, 1, Y), f32), pltpu.VMEM((slots, NS, 1, Y), f32),
                pltpu.VMEM((OUTER, 1, Y), f32), pltpu.VMEM((OUTER, NPD, 1, Y), f32),
                pltpu.VMEM((2, 1, Y), jnp.int32),
                plane(5, T), plane(2), plane(2), dma((3,)),
                dma((2, 3)), dma((2, 3)), dma((2, 2, STEPS)), dma((2, 2, STEPS)),
                dma((STEPS, far)), dma((STEPS, far)), dma((STEPS, far)), dma((STEPS, far)),
                dma((slots, NS - 1)), dma((slots, NS - 1)), dma((OUTER, far)), dma((OUTER, far)),
            ],
            compiler_params=pltpu.CompilerParams(collective_id=0, has_side_effects=True),
        )(u, prec, bound, cap, capacity, bv, tc, dens, slope, om)

    in_specs = (
        P("strip", "period", None, None),
        P(None, "strip", "period", None, None),
        P("strip", "period", None, None),
        P("period"),
        P("period"),
        P("strip", None, None),
        P("strip", None, None),
        P(),
        P("strip", None),
        P(),
    )
    out_specs = (
        P("strip", "period", None, None),
        P(None, "strip", "period", None, None),
        P("strip", "period", None, None),
        P("period"),
        P(),
    )
    return jax.shard_map(
        per_device, mesh=mesh, in_specs=in_specs, out_specs=out_specs, check_vma=False
    )
```
